32 devices in a mesh: group: 2 (over x), vocab: 16 (over z, y, core).
Axes of the slice: x: 2, y: 2, z: 4, core: 2. Of those that a mesh axis runs over, the one named last changes fastest.
Arguments:
- table: bfloat16 [4608, 12288], P('vocab', 'group')
- hidden: bfloat16 [448, 4608], P(None, 'vocab')
- gain: bfloat16 [4608], P('vocab'), may hold values from 0.099609375 to 1.8984375
- ids: int32 [448], replicated, may hold values from 0 to 12287
Outputs:
- next_embed: bfloat16 [448, 4608], P(None, 'vocab')
- logprobs: float32 [448, 12288], P(None, ('group', 'vocab'))
- chosen: float32 [448], replicated
The draws below stay inside these ranges and needn't reach their ends.
All inputs are finite; a program needn't handle non-finite values.
Results may differ from the reference program's by a relative error of at most 0.001.
Values may be sent and summed in bfloat16 or wider, within the bound.
A program may use at most 64 MiB of HBM per device.

```python
import math
import jax
import jax.numpy as jnp
from jax import lax

D = 4608
TOK = 448
VOCAB = 12288


def draw_table(key, part):
    first, second = jax.random.split(jax.random.fold_in(key, 11))
    place = jnp.arange(VOCAB, dtype=jnp.float32) / VOCAB
    rough = jnp.exp(jax.random.uniform(second, (VOCAB,), jnp.float32, -0.35, 0.35))
    base = jax.random.normal(first, (D, VOCAB), jnp.float32)
    scale = 0.5 * 4.0 ** place * rough
    return (base * scale[None, :] / math.sqrt(D)).astype(jnp.bfloat16)


def draw_hidden(key, part):
    first, second, third = jax.random.split(jax.random.fold_in(key, 23), 3)
    place = jnp.arange(D, dtype=jnp.float32) / D
    rough = jnp.exp(jax.random.uniform(second, (D,), jnp.float32, -0.5, 0.5))
    row_scale = 10.0 ** jax.random.uniform(third, (TOK, 1), jnp.float32, 0.0, 1.0)
    base = jax.random.normal(first, (TOK, D), jnp.float32)
    column = 10.0 ** place * rough
    return (base * column[None, :] * row_scale).astype(jnp.bfloat16)


def touch_ends(result, key, smallest, top_value):
    longest = result.shape.index(max(result.shape))
    spots = []
    for shift in (0, 1):
        where = [jax.random.randint(jax.random.fold_in(key, axis), (), 0, length) for axis, length in enumerate(result.shape)]
        where[longest] = (where[longest] + shift) % result.shape[longest]
        spots.append(tuple(where))
    return result.at[spots[0]].set(smallest).at[spots[1]].set(top_value)


def setup_inputs(seed: int = 0) -> dict:
    key_of = jax.random.split(jax.random.key(seed), 5)
    table = draw_table(jax.random.fold_in(key_of[4], 71), 0)
    hidden = draw_hidden(jax.random.fold_in(key_of[4], 71), 0)
    gain = jnp.clip(1.0 + 0.18 * jax.random.normal(key_of[2], (D,), jnp.float32), 0.099609375, 1.8984375).astype(jnp.bfloat16)
    ids = touch_ends(jax.random.randint(key_of[3], (TOK,), 0, VOCAB), jax.random.fold_in(key_of[3], 1), 0, VOCAB - 1).astype(jnp.int32)
    return {"table": table, "hidden": hidden, "gain": gain, "ids": ids}


def reference(table, hidden, gain, ids):
    picked = jnp.take(table, ids, axis=1).astype(jnp.float32).T
    next_embed = (picked * math.sqrt(D)).astype(jnp.bfloat16)
    states = hidden.astype(jnp.float32)
    mean_sq = lax.optimization_barrier(jnp.sum(states * states, axis=1, keepdims=True)) / D
    normed = (states * gain.astype(jnp.float32) * lax.rsqrt(mean_sq + 1e-06)).astype(jnp.bfloat16)
    logits = jnp.dot(normed, table, preferred_element_type=jnp.float32)
    capped = 30.0 * jnp.tanh(logits / 30.0)
    total = lax.optimization_barrier(jnp.sum(jnp.exp(capped), axis=1))
    log_total = jnp.log(total)
    logprobs = capped - log_total[:, None]
    picked_logit = jnp.take_along_axis(capped, ids[:, None].astype(jnp.int32), axis=1)[:, 0]
    chosen = picked_logit - log_total
    return (next_embed, logprobs, chosen)
```

```python
import functools
import math

import jax
import jax.numpy as jnp
from jax import lax
from jax.experimental import pallas as pl
from jax.experimental.pallas import tpu as pltpu
from jax.sharding import PartitionSpec as P

MESH = pl.DeviceIdType.MESH
NT = (((1,), (1,)), ((), ()))
HIGH = lax.Precision.HIGHEST


def peers_order(nz):
    ks = sorted(range(1, nz), key=lambda k: -min(k, nz - k))
    return ks + [0]


def kernel(
    sizes, table, hidden, gain, ids, embed_out, capped_out, stats_out,
    tab_v, tpar, hpar, gpar, own_n, par_n, ysend, yrecv, zsend, zrecv, acc,
    xsend, xrecv, found, msend, mrecv, ssend, srecv, local_sem, send_sem, recv_sem,
):
    groups, share, width, n_tok, span, voc_cols, nz = sizes
    g = lax.axis_index("group")
    v = lax.axis_index("vocab")
    c, y, z = lax.rem(v, 2), lax.rem(v // 2, 2), v // 4
    core_peer = (g, v + 1 - 2 * c)
    y_peer = (g, v + 2 - 4 * y)

    def z_peer(k):
        return (g, lax.rem(z + k, nz) * 4 + y * 2 + c)

    def g_peer(d):
        return (lax.rem(g + d, groups), v)

    def column(zz, yy, cc):
        return pl.ds(pl.multiple_of((zz * 4 + yy * 2 + cc) * voc_cols, 128), voc_cols)

    order = peers_order(nz)
    started = []

    def send(src, dst, peer):
        i = len(started)
        copy = pltpu.make_async_remote_copy(
            src_ref=src, dst_ref=dst, send_sem=send_sem.at[i], recv_sem=recv_sem.at[i],
            device_id=peer, device_id_type=MESH,
        )
        copy.start()
        started.append(copy)
        return copy

    load = pltpu.make_async_copy(table, tab_v, local_sem)
    load.start()

    barrier = pltpu.get_barrier_semaphore()
    everyone = [core_peer, y_peer]
    everyone += [z_peer(k) for k in range(1, nz)]
    everyone += [g_peer(d) for d in range(1, groups)]
    for peer in everyone:
        pl.semaphore_signal(barrier, inc=1, device_id=peer, device_id_type=MESH)

    states = hidden[...].astype(jnp.float32)
    ones = jnp.ones((8, share), jnp.float32)
    sq = lax.dot_general(ones, states * states, NT, precision=HIGH,
                         preferred_element_type=jnp.float32)
    msend[0] = sq
    pl.semaphore_wait(barrier, len(everyone))

    first_ms = send(msend.at[0], mrecv.at[0], core_peer)
    h_copy = send(hidden, hpar, core_peer)
    g_copy = send(gain, gpar, core_peer)
    t_copies = []
    for i, k in enumerate(order):
        zz = lax.rem(z + k, nz)
        for half, yy in enumerate((1 - y, y)):
            t_copies.append(send(table.at[:, column(zz, yy, 1 - c)], tpar.at[2 * i + half], core_peer))

    first_ms.wait_recv()
    sq = sq + mrecv[0]
    msend[1] = sq
    send(msend.at[1], mrecv.at[1], y_peer).wait_recv()
    sq = sq + mrecv[1]
    msend[2] = sq
    copies = [send(msend.at[2], mrecv.at[1 + k], z_peer(k)) for k in range(1, nz)]
    for k, copy in enumerate(copies):
        copy.wait_recv()
        sq = sq + mrecv[2 + k]
    scale = lax.rsqrt(sq / width + 1e-06).T[:, :1]

    own_n[...] = (states * gain[...] * scale).astype(jnp.bfloat16)
    h_copy.wait_recv()
    g_copy.wait_recv()
    par_n[...] = (hpar[...].astype(jnp.float32) * gpar[...] * scale).astype(jnp.bfloat16)
    load.wait()

    def partial(i, half, zz, yy):
        t_copies[2 * i + half].wait_recv()
        first = jnp.dot(own_n[...], tab_v[:, column(zz, yy, c)], preferred_element_type=jnp.float32)
        return first + jnp.dot(par_n[...], tpar[2 * i + half], preferred_element_type=jnp.float32)

    y_copies = []
    for i, k in enumerate(order):
        zz = lax.rem(z + k, nz)
        ysend[i] = partial(i, 0, zz, 1 - y).astype(jnp.bfloat16)
        y_copies.append(send(ysend.at[i], yrecv.at[i], y_peer))

    chunk = 2 * voc_cols
    inside = ids[...] - g * span
    found[...] = jnp.zeros_like(found)

    def gather(n, carry):
        start = n * chunk
        places = lax.broadcasted_iota(jnp.int32, (n_tok, chunk), 1)
        hot = jnp.where(places == inside - start, 1.0, 0.0).astype(jnp.bfloat16)
        found[...] += lax.dot_general(
            hot, tab_v[:, pl.ds(pl.multiple_of(start, 128), chunk)], NT,
            preferred_element_type=jnp.float32)
        return carry

    lax.fori_loop(0, span // chunk, gather, 0)
    xsend[...] = found[...].astype(jnp.bfloat16)
    x_copies = [send(xsend, xrecv.at[d - 1], g_peer(d)) for d in range(1, groups)]

    z_copies = {}
    for i, k in enumerate(order):
        zz = lax.rem(z + k, nz)
        both = partial(i, 1, zz, y)
        y_copies[i].wait_recv()
        both = both + yrecv[i].astype(jnp.float32)
        if k:
            zsend[k - 1] = both.astype(jnp.bfloat16)
            z_copies[k] = send(zsend.at[k - 1], zrecv.at[k - 1], z_peer(k))
        else:
            acc[...] = both

    embed = found[...]
    for d, copy in enumerate(x_copies):
        copy.wait_recv()
        embed = embed + xrecv[d].astype(jnp.float32)
    embed_out[...] = embed.astype(jnp.bfloat16)

    logits = acc[...]
    for k in order[:-1]:
        z_copies[k].wait_recv()
        logits = logits + zrecv[k - 1].astype(jnp.float32)
    capped = 30.0 * jnp.tanh(logits / 30.0)
    capped_out[...] = capped
    first_col = (g * 4 * nz + v) * voc_cols
    places = lax.broadcasted_iota(jnp.int32, (n_tok, voc_cols), 1)
    pick = jnp.where(places == ids[...] - first_col, capped, 0.0)
    ones = jnp.ones((8, voc_cols), jnp.float32)
    sums = lax.dot_general(ones, jnp.exp(capped), NT, precision=HIGH,
                           preferred_element_type=jnp.float32)
    picks = lax.dot_general(ones, pick, NT, precision=HIGH,
                            preferred_element_type=jnp.float32)
    slot = 0
    stages = [[core_peer], [y_peer], [z_peer(k) for k in range(1, nz)],
              [g_peer(d) for d in range(1, groups)]]
    for stage, peers in enumerate(stages):
        ssend[stage, 0] = sums
        ssend[stage, 1] = picks
        copies = []
        for peer in peers:
            copies.append((slot, send(ssend.at[stage], srecv.at[slot], peer)))
            slot += 1
        for at, copy in copies:
            copy.wait_recv()
            sums = sums + srecv[at, 0]
            picks = picks + srecv[at, 1]
    stats_out[0] = sums
    stats_out[1] = picks
    for copy in started:
        copy.wait_send()


def body(table, hidden, gain, ids):
    share, span = table.shape
    n_tok = hidden.shape[0]
    vocab_n = lax.axis_size("vocab")
    groups = lax.axis_size("group")
    voc_cols = span // vocab_n
    width = share * vocab_n
    nz = vocab_n // 4
    half = vocab_n // 2
    peers = 2 + (nz - 1) + (groups - 1)
    n_copies = (nz + 1) + 2 + half + nz + (groups - 1) + (nz - 1) + peers
    bf16, f32 = jnp.bfloat16, jnp.float32
    sizes = (groups, share, width, n_tok, span, voc_cols, nz)
    vmem = pl.BlockSpec(memory_space=pltpu.VMEM)
    found, capped, stats = pl.pallas_call(
        functools.partial(kernel, sizes),
        out_shape=(
            jax.ShapeDtypeStruct((n_tok, share), bf16),
            jax.ShapeDtypeStruct((n_tok, voc_cols), f32),
            jax.ShapeDtypeStruct((2, 8, n_tok), f32),
        ),
        in_specs=[pl.BlockSpec(memory_space=pl.ANY), vmem, vmem, vmem],
        out_specs=(vmem, vmem, vmem),
        scratch_shapes=[
            pltpu.VMEM((share, span), bf16),
            pltpu.VMEM((half, share, voc_cols), bf16),
            pltpu.VMEM((n_tok, share), bf16),
            pltpu.VMEM((1, share), f32),
            pltpu.VMEM((n_tok, share), bf16),
            pltpu.VMEM((n_tok, share), bf16),
            pltpu.VMEM((nz, n_tok, voc_cols), bf16),
            pltpu.VMEM((nz, n_tok, voc_cols), bf16),
            pltpu.VMEM((nz - 1, n_tok, voc_cols), bf16),
            pltpu.VMEM((nz - 1, n_tok, voc_cols), bf16),
            pltpu.VMEM((n_tok, voc_cols), f32),
            pltpu.VMEM((n_tok, share), bf16),
            pltpu.VMEM((groups - 1, n_tok, share), bf16),
            pltpu.VMEM((n_tok, share), f32),
            pltpu.VMEM((3, 8, n_tok), f32),
            pltpu.VMEM((nz + 1, 8, n_tok), f32),
            pltpu.VMEM((4, 2, 8, n_tok), f32),
            pltpu.VMEM((peers, 2, 8, n_tok), f32),
            pltpu.SemaphoreType.DMA,
            pltpu.SemaphoreType.DMA((n_copies,)),
            pltpu.SemaphoreType.DMA((n_copies,)),
        ],
        compiler_params=pltpu.CompilerParams(
            collective_id=0, has_side_effects=True, vmem_limit_bytes=60 * 1024 * 1024
        ),
    )(table, hidden, gain.astype(f32)[None, :], ids[:, None])
    next_embed = (found.astype(f32) * math.sqrt(width)).astype(bf16)
    log_total = jnp.log(stats[0, 0])
    logprobs = capped - log_total[:, None]
    chosen = stats[1, 0] - log_total
    return (next_embed, logprobs, chosen)


def solution(mesh):
    placed = (P("vocab", "group"), P(None, "vocab"), P("vocab"), P())
    return jax.shard_map(
        body,
        mesh=mesh,
        in_specs=placed,
        out_specs=(P(None, "vocab"), P(None, ("group", "vocab")), P()),
        check_vma=False,
    )
```

```python
import functools
import math

import jax
import jax.numpy as jnp
from jax import lax
from jax.experimental import pallas as pl
from jax.experimental.pallas import tpu as pltpu
from jax.sharding import PartitionSpec as P

MESH = pl.DeviceIdType.MESH


def stage_bits(half, bits):
    dims = list(range(bits))
    if half == 0:
        dims[0], dims[1] = dims[1], dims[0]
    return [1 << d for d in dims]


def stage_of(half, mask, bits):
    for stage, bit in enumerate(stage_bits(half, bits)):
        if mask & bit:
            return stage
    return bits


def program_order(bits):
    if bits == 3:
        return [(1, 7), (0, 7), (0, 6), (1, 5), (0, 3), (0, 2), (0, 5), (1, 3), (0, 1), (1, 1),
                None, (1, 6), (1, 4), (0, 4), (1, 2)]
    every = [(half, mask) for mask in range((1 << bits) - 1, 0, -1) for half in (1, 0)]
    every.sort(key=lambda one: stage_of(one[0], one[1], bits))
    return every + [None]


def kernel(
    sizes, table, hidden, gain, ids, embed_out, capped_out, stats_out,
    tab_v, tpar, hown, hpar, gpar, own_n, par_n, send0, recv0, send1, recv1,
    xsend, xrecv, found, msend, mrecv, ssend, srecv, local_sem, send_sem, recv_sem,
):
    groups, share, width, n_tok, span, voc_cols, nz, bits, split = sizes
    f32, bf16 = jnp.float32, jnp.bfloat16
    g = lax.axis_index("group")
    v = lax.axis_index("vocab")
    c, y, z = v % 2, (v // 2) % 2, v // 4
    rows = ((0, split), (split, n_tok))
    sends, recvs = (send0, send1), (recv0, recv1)

    def flip(value, on):
        return 1 - value if on else value

    def place(mask, core):
        zz = 0
        for i in range(bits - 1):
            zz = zz + (1 << i) * flip((z // (1 << i)) % 2, (mask >> (i + 1)) & 1)
        return zz * 4 + flip(y, mask & 1) * 2 + core

    def z_peer(k):
        return (g, ((z + k) % nz) * 4 + y * 2 + c)

    def near_peer(d, m):
        gg = (g + d) % groups if d else g
        return (gg, z * 4 + flip(y, m & 1) * 2 + flip(c, m & 2))

    core_peer = near_peer(0, 2)
    z_peers = [z_peer(k) for k in range(1, nz)]
    near_vocab = [near_peer(0, m) for m in range(1, 4)]
    near_all = near_vocab + [near_peer(d, m) for d in range(1, groups) for m in range(4)]

    def column(mask, core):
        return pl.ds(pl.multiple_of(place(mask, core) * voc_cols, 128), voc_cols)

    started = []

    def send(src, dst, peer):
        i = len(started)
        copy = pltpu.make_async_remote_copy(
            src_ref=src, dst_ref=dst, send_sem=send_sem.at[i], recv_sem=recv_sem.at[i],
            device_id=peer, device_id_type=MESH,
        )
        copy.start()
        started.append(copy)
        return copy

    h_load = pltpu.make_async_copy(hidden, hown, local_sem.at[0])
    h_load.start()
    load = pltpu.make_async_copy(table, tab_v, local_sem.at[1])
    load.start()

    barrier = pltpu.get_barrier_semaphore()
    everyone = z_peers + near_all
    for peer in everyone:
        pl.semaphore_signal(barrier, inc=1, device_id=peer, device_id_type=MESH)

    h_load.wait()
    states = hown[...].astype(f32)
    sq = jnp.broadcast_to(jnp.sum(states * states, axis=0, keepdims=True), (8, n_tok))
    msend[0] = sq
    own_t = states.T * gain[...].astype(f32).reshape(1, share)
    pl.semaphore_wait(barrier, len(everyone))

    copies = [send(msend.at[0], mrecv.at[j], peer) for j, peer in enumerate(z_peers)]
    h_copy = send(hidden, hpar, core_peer)
    g_copy = send(gain, gpar, core_peer)
    order = program_order(bits)
    uses = []
    for one in order:
        if one and one[1] not in uses:
            uses.append(one[1])
    t_copies = {}
    for mask in uses + [0]:
        t_copies[mask] = send(table.at[:, column(mask, 1 - c)], tpar.at[mask], core_peer)

    h_copy.wait_recv()
    g_copy.wait_recv()
    par_t = hpar[...].astype(f32).T * gpar[...].astype(f32).reshape(1, share)

    for j, copy in enumerate(copies):
        copy.wait_recv()
        sq = sq + mrecv[j]
    msend[1] = sq
    copies = [send(msend.at[1], mrecv.at[nz - 1 + j], peer) for j, peer in enumerate(near_vocab)]
    for j, copy in enumerate(copies):
        copy.wait_recv()
        sq = sq + mrecv[nz - 1 + j]
    scale = lax.rsqrt(sq / width + 1e-06).T[:, :1]
    own_n[...] = (own_t * scale).astype(bf16)
    par_n[...] = (par_t * scale).astype(bf16)
    load.wait()

    landed = set()

    def partial(half, mask):
        if mask not in landed:
            t_copies[mask].wait_recv()
            landed.add(mask)
        low, high = rows[half]
        first = jnp.dot(own_n[low:high], tab_v[:, column(mask, c)], preferred_element_type=f32)
        return first + jnp.dot(par_n[low:high], tpar[mask], preferred_element_type=f32)

    arrivals = {}

    def reduced(half, mask):
        total = partial(half, mask)
        for bit in stage_bits(half, bits)[:stage_of(half, mask, bits)]:
            arrivals[half, mask | bit].wait_recv()
            total = total + recvs[half][(mask | bit) - 1].astype(f32)
        return total

    chunk = 2 * voc_cols
    local_ids = ids[...].reshape(1, n_tok) - g * span

    def gather(n, carry):
        start = n * chunk
        spots = lax.broadcasted_iota(jnp.int32, (chunk, n_tok), 0)
        hot = jnp.where(spots == local_ids - start, 1.0, 0.0).astype(bf16)
        found[...] += jnp.dot(tab_v[:, pl.ds(pl.multiple_of(start, 128), chunk)], hot,
                              preferred_element_type=f32)
        return carry

    x_copies = []
    for one in order:
        if one is None:
            found[...] = jnp.zeros_like(found)
            lax.fori_loop(0, span // chunk, gather, 0)
            xsend[...] = found[...].astype(bf16)
            x_copies = [send(xsend, xrecv.at[d - 1], near_peer(d, 0)) for d in range(1, groups)]
            continue
        half, mask = one
        sends[half][mask - 1] = reduced(half, mask).astype(bf16)
        bit = stage_bits(half, bits)[stage_of(half, mask, bits)]
        peer = (g, place(bit, c))
        arrivals[half, mask] = send(sends[half].at[mask - 1], recvs[half].at[mask - 1], peer)

    embed = found[...]
    for d, copy in enumerate(x_copies):
        copy.wait_recv()
        embed = embed + xrecv[d].astype(f32)
    embed_out[...] = (embed * math.sqrt(width)).astype(bf16)

    first_col = (g * 4 * nz + v) * voc_cols
    offsets = jnp.broadcast_to(ids[...].reshape(1, n_tok), (8, n_tok)).astype(f32).T[:, :1].astype(jnp.int32)
    sums, picks = [], []
    for half, (low, high) in enumerate(rows):
        capped = 30.0 * jnp.tanh(reduced(half, 0) / 30.0)
        capped_out[low:high] = capped
        spots = lax.broadcasted_iota(jnp.int32, capped.shape, 1)
        pick = jnp.where(spots == offsets[low:high] - first_col, capped, 0.0)
        sums.append(jnp.sum(jnp.exp(capped), axis=1, keepdims=True))
        picks.append(jnp.sum(pick, axis=1, keepdims=True))
    sums = jnp.broadcast_to(jnp.concatenate(sums, axis=0), (n_tok, 8)).T
    picks = jnp.broadcast_to(jnp.concatenate(picks, axis=0), (n_tok, 8)).T
    slot = 0
    for phase, peers in enumerate((z_peers, near_all)):
        ssend[phase, 0] = sums
        ssend[phase, 1] = picks
        copies = []
        for peer in peers:
            copies.append((slot, send(ssend.at[phase], srecv.at[slot], peer)))
            slot += 1
        for at, copy in copies:
            copy.wait_recv()
            sums = sums + srecv[at, 0]
            picks = picks + srecv[at, 1]
    stats_out[0] = sums
    stats_out[1] = picks
    for copy in started:
        copy.wait_send()


def finish(embed, capped, stats, embed_out, logprobs_out, chosen_out):
    log_total = jnp.log(stats[0])
    embed_out[...] = embed[...]
    logprobs_out[...] = capped[...] - log_total.T[:, :1]
    chosen_out[...] = (stats[1] - log_total)[:1]


def body(table, hidden, gain, ids):
    share, span = table.shape
    n_tok = hidden.shape[0]
    vocab_n = lax.axis_size("vocab")
    groups = lax.axis_size("group")
    voc_cols = span // vocab_n
    width = share * vocab_n
    nz = vocab_n // 4
    half = vocab_n // 2
    bits = half.bit_length() - 1
    split = n_tok // 64 * 16
    near = 3 + 4 * (groups - 1)
    n_copies = (nz - 1) + 3 + 2 + half + 2 * (half - 1) + (groups - 1) + (nz - 1) + near
    bf16, f32 = jnp.bfloat16, jnp.float32
    sizes = (groups, share, width, n_tok, span, voc_cols, nz, bits, split)
    vmem = pl.BlockSpec(memory_space=pltpu.VMEM)
    anywhere = pl.BlockSpec(memory_space=pl.ANY)
    embed, capped, stats = pl.pallas_call(
        functools.partial(kernel, sizes),
        out_shape=(
            jax.ShapeDtypeStruct((share, n_tok), bf16),
            jax.ShapeDtypeStruct((n_tok, voc_cols), f32),
            jax.ShapeDtypeStruct((2, 8, n_tok), f32),
        ),
        in_specs=[anywhere, anywhere, vmem, vmem],
        out_specs=(vmem, vmem, vmem),
        scratch_shapes=[
            pltpu.VMEM((share, span), bf16),
            pltpu.VMEM((half, share, voc_cols), bf16),
            pltpu.VMEM((share, n_tok), bf16),
            pltpu.VMEM((share, n_tok), bf16),
            pltpu.VMEM((share,), bf16),
            pltpu.VMEM((n_tok, share), bf16),
            pltpu.VMEM((n_tok, share), bf16),
            pltpu.VMEM((half - 1, split, voc_cols), bf16),
            pltpu.VMEM((half - 1, split, voc_cols), bf16),
            pltpu.VMEM((half - 1, n_tok - split, voc_cols), bf16),
            pltpu.VMEM((half - 1, n_tok - split, voc_cols), bf16),
            pltpu.VMEM((share, n_tok), bf16),
            pltpu.VMEM((groups - 1, share, n_tok), bf16),
            pltpu.VMEM((share, n_tok), f32),
            pltpu.VMEM((2, 8, n_tok), f32),
            pltpu.VMEM((nz + 2, 8, n_tok), f32),
            pltpu.VMEM((2, 2, 8, n_tok), f32),
            pltpu.VMEM((nz - 1 + near, 2, 8, n_tok), f32),
            pltpu.SemaphoreType.DMA((2,)),
            pltpu.SemaphoreType.DMA((n_copies,)),
            pltpu.SemaphoreType.DMA((n_copies,)),
        ],
        compiler_params=pltpu.CompilerParams(
            collective_id=0, has_side_effects=True, vmem_limit_bytes=60 * 1024 * 1024
        ),
    )(table, hidden.T, gain, ids)
    next_embed, logprobs, chosen = pl.pallas_call(
        finish,
        out_shape=(
            jax.ShapeDtypeStruct((share, n_tok), bf16),
            jax.ShapeDtypeStruct((n_tok, voc_cols), f32),
            jax.ShapeDtypeStruct((1, n_tok), f32),
        ),
        in_specs=[vmem] * 3,
        out_specs=(vmem,) * 3,
    )(embed, capped, stats)
    return (next_embed.T, logprobs, chosen[0])


def solution(mesh):
    placed = (P("vocab", "group"), P(None, "vocab"), P("vocab"), P())
    return jax.shard_map(
        body,
        mesh=mesh,
        in_specs=placed,
        out_specs=(P(None, "vocab"), P(None, ("group", "vocab")), P()),
        check_vma=False,
    )
```

```python
import functools
import math

import jax
import jax.numpy as jnp
from jax import lax
from jax.experimental import pallas as pl
from jax.experimental.pallas import tpu as pltpu
from jax.sharding import PartitionSpec as P

MESH = pl.DeviceIdType.MESH


def stage_bits(half, bits):
    dims = list(range(bits))
    if half == 0:
        dims[0], dims[1] = dims[1], dims[0]
    return [1 << d for d in dims]


def stage_of(half, mask, bits):
    for stage, bit in enumerate(stage_bits(half, bits)):
        if mask & bit:
            return stage
    return bits


def program_order(bits):
    if bits == 3:
        return [(1, 7), (0, 7), (0, 6), (1, 5), (0, 3), (0, 2), (0, 5), (1, 3), (0, 1), (1, 1),
                None, (1, 6), (1, 4), (0, 4), (1, 2)]
    every = [(half, mask) for mask in range((1 << bits) - 1, 0, -1) for half in (1, 0)]
    every.sort(key=lambda one: stage_of(one[0], one[1], bits))
    return every + [None]


def kernel(
    sizes, table, hidden, gain, ids, embed_out, capped_out, stats_out,
    tab_v, tpar, hown, hpar, gpar, own_n, par_n, send0, recv0, send1, recv1,
    xsend, xrecv, found, msend, mrecv, ssend, srecv, local_sem, send_sem, recv_sem,
):
    groups, share, width, n_tok, span, voc_cols, nz, bits, split = sizes
    f32, bf16 = jnp.float32, jnp.bfloat16
    g = lax.axis_index("group")
    v = lax.axis_index("vocab")
    c, y, z = v % 2, (v // 2) % 2, v // 4
    rows = ((0, split), (split, n_tok))
    sends, recvs = (send0, send1), (recv0, recv1)

    def flip(value, on):
        return 1 - value if on else value

    def place(mask, core):
        zz = 0
        for i in range(bits - 1):
            zz = zz + (1 << i) * flip((z // (1 << i)) % 2, (mask >> (i + 1)) & 1)
        return zz * 4 + flip(y, mask & 1) * 2 + core

    def z_peer(k):
        return (g, ((z + k) % nz) * 4 + y * 2 + c)

    def near_peer(d, m):
        gg = (g + d) % groups if d else g
        return (gg, z * 4 + flip(y, m & 1) * 2 + flip(c, m & 2))

    core_peer = near_peer(0, 2)
    z_peers = [z_peer(k) for k in range(1, nz)]
    near_all = [near_peer(0, m) for m in range(1, 4)] + [near_peer(d, m) for d in range(1, groups) for m in range(4)]

    def column(mask, core):
        return pl.ds(pl.multiple_of(place(mask, core) * voc_cols, 128), voc_cols)

    started = []

    def send(src, dst, peer):
        i = len(started)
        copy = pltpu.make_async_remote_copy(
            src_ref=src, dst_ref=dst, send_sem=send_sem.at[i], recv_sem=recv_sem.at[i],
            device_id=peer, device_id_type=MESH,
        )
        copy.start()
        started.append(copy)
        return copy

    h_load = pltpu.make_async_copy(hidden, hown, local_sem.at[0])
    h_load.start()
    load = pltpu.make_async_copy(table, tab_v, local_sem.at[1])
    load.start()

    barrier = pltpu.get_barrier_semaphore()
    chip_peers = [(g, place(m, c)) for m in range(1, 2 * nz)]
    everyone = chip_peers + [peer for m, peer in enumerate(near_all) if m != 0]
    for peer in everyone:
        pl.semaphore_signal(barrier, inc=1, device_id=peer, device_id_type=MESH)

    h_load.wait()
    states = hown[...].astype(f32)
    own_sq = jnp.sum(states * states, axis=0, keepdims=True)
    own_t = states.T * gain[...].astype(f32).reshape(1, share)
    pl.semaphore_wait(barrier, len(everyone))

    h_copy = send(hidden, hpar, core_peer)
    g_copy = send(gain, gpar, core_peer)
    order = program_order(bits)
    uses = []
    for one in order:
        if one and one[1] not in uses:
            uses.append(one[1])
    t_copies = {}
    for mask in uses + [0]:
        t_copies[mask] = send(table.at[:, column(mask, 1 - c)], tpar.at[mask], core_peer)

    h_copy.wait_recv()
    states = hpar[...].astype(f32)
    chip_sq = own_sq + jnp.sum(states * states, axis=0, keepdims=True)
    msend[...] = chip_sq
    sq_copies = [send(msend, mrecv.at[j], peer) for j, peer in enumerate(chip_peers)]

    def to_columns(row_list):
        full = jnp.concatenate(row_list + [row_list[0]] * (8 - len(row_list)), axis=0)
        full = full.T
        return [full[:, i:i + 1] for i in range(len(row_list))]

    chip_scale = to_columns([lax.rsqrt(chip_sq / width + 1e-06)])[0]
    own_n[...] = (own_t * chip_scale).astype(bf16)
    g_copy.wait_recv()
    par_t = states.T * gpar[...].astype(f32).reshape(1, share)
    par_n[...] = (par_t * chip_scale).astype(bf16)
    load.wait()

    ratios = []

    def ratio_columns():
        if not ratios:
            total = chip_sq
            for j, copy in enumerate(sq_copies):
                copy.wait_recv()
                total = total + mrecv[j]
            scale = lax.rsqrt(total / width + 1e-06)
            parts = [chip_sq, mrecv[0], mrecv[1]]
            ratios.extend(to_columns([
                jnp.where(scale == 0.0, 0.0, scale * jnp.sqrt(part / width + 1e-06))
                for part in parts]))
        return ratios

    landed = set()

    def partial(half, mask):
        if mask not in landed:
            t_copies[mask].wait_recv()
            landed.add(mask)
        low, high = rows[half]
        first = jnp.dot(own_n[low:high], tab_v[:, column(mask, c)], preferred_element_type=f32)
        return first + jnp.dot(par_n[low:high], tpar[mask], preferred_element_type=f32)

    arrivals = {}

    def reduced(half, mask):
        total = partial(half, mask)
        stage = stage_of(half, mask, bits)
        if stage == 0:
            return total
        low, high = rows[half]
        own, by_y, by_z = ratio_columns()
        total = total * own[low:high]
        for i, bit in enumerate(stage_bits(half, bits)[:stage]):
            arrivals[half, mask | bit].wait_recv()
            more = recvs[half][(mask | bit) - 1].astype(f32)
            if i == 0:
                more = more * (by_y if half else by_z)[low:high]
            total = total + more
        return total

    chunk = 2 * voc_cols
    local_ids = ids[...].reshape(1, n_tok) - g * span

    def gather(n, carry):
        start = n * chunk
        spots = lax.broadcasted_iota(jnp.int32, (chunk, n_tok), 0)
        hot = jnp.where(spots == local_ids - start, 1.0, 0.0).astype(bf16)
        found[...] += jnp.dot(tab_v[:, pl.ds(pl.multiple_of(start, 128), chunk)], hot,
                              preferred_element_type=f32)
        return carry

    x_copies = []
    for one in order:
        if one is None:
            found[...] = jnp.zeros_like(found)
            lax.fori_loop(0, span // chunk, gather, 0)
            xsend[...] = found[...].astype(bf16)
            x_copies = [send(xsend, xrecv.at[d - 1], near_peer(d, 0)) for d in range(1, groups)]
            continue
        half, mask = one
        sends[half][mask - 1] = reduced(half, mask).astype(bf16)
        bit = stage_bits(half, bits)[stage_of(half, mask, bits)]
        peer = (g, place(bit, c))
        arrivals[half, mask] = send(sends[half].at[mask - 1], recvs[half].at[mask - 1], peer)

    embed = found[...]
    for d, copy in enumerate(x_copies):
        copy.wait_recv()
        embed = embed + xrecv[d].astype(f32)
    embed_out[...] = (embed * math.sqrt(width)).astype(bf16)

    first_col = (g * 4 * nz + v) * voc_cols
    offsets = jnp.broadcast_to(ids[...].reshape(1, n_tok), (8, n_tok)).astype(f32).T[:, :1].astype(jnp.int32)
    sums, picks = [], []
    for half, (low, high) in enumerate(rows):
        capped = 30.0 * jnp.tanh(reduced(half, 0) / 30.0)
        capped_out[low:high] = capped
        spots = lax.broadcasted_iota(jnp.int32, capped.shape, 1)
        pick = jnp.where(spots == offsets[low:high] - first_col, capped, 0.0)
        sums.append(jnp.sum(jnp.exp(capped), axis=1, keepdims=True))
        picks.append(jnp.sum(pick, axis=1, keepdims=True))
    both = [jnp.broadcast_to(jnp.concatenate(one, axis=0), (n_tok, 8)).T[:1] for one in (sums, picks)]
    both = jnp.concatenate(both, axis=0)
    slot = 0
    for phase, peers in enumerate((z_peers, near_all)):
        ssend[phase] = both
        copies = []
        for peer in peers:
            copies.append((slot, send(ssend.at[phase], srecv.at[slot], peer)))
            slot += 1
        for at, copy in copies:
            copy.wait_recv()
            both = both + srecv[at]
    stats_out[...] = both
    for copy in started:
        copy.wait_send()


def finish(embed, capped, stats, embed_out, logprobs_out, chosen_out):
    log_total = jnp.log(stats[0:1])
    embed_out[...] = embed[...]
    logprobs_out[...] = capped[...] - jnp.broadcast_to(log_total, (8, log_total.shape[1])).T[:, :1]
    chosen_out[...] = stats[1:2] - log_total


def body(table, hidden, gain, ids):
    share, span = table.shape
    n_tok = hidden.shape[0]
    vocab_n = lax.axis_size("vocab")
    groups = lax.axis_size("group")
    voc_cols = span // vocab_n
    width = share * vocab_n
    nz = vocab_n // 4
    half = vocab_n // 2
    bits = half.bit_length() - 1
    split = n_tok // 64 * 16
    near = 3 + 4 * (groups - 1)
    n_copies = 2 + half + 3 * (half - 1) + (groups - 1) + (nz - 1) + near
    bf16, f32 = jnp.bfloat16, jnp.float32
    sizes = (groups, share, width, n_tok, span, voc_cols, nz, bits, split)
    vmem = pl.BlockSpec(memory_space=pltpu.VMEM)
    anywhere = pl.BlockSpec(memory_space=pltpu.HBM)
    embed, capped, stats = pl.pallas_call(
        functools.partial(kernel, sizes),
        out_shape=(
            jax.ShapeDtypeStruct((share, n_tok), bf16),
            jax.ShapeDtypeStruct((n_tok, voc_cols), f32),
            jax.ShapeDtypeStruct((2, n_tok), f32),
        ),
        in_specs=[anywhere, anywhere, vmem, vmem],
        out_specs=(vmem, vmem, vmem),
        scratch_shapes=[
            pltpu.VMEM((share, span), bf16),
            pltpu.VMEM((half, share, voc_cols), bf16),
            pltpu.VMEM((share, n_tok), bf16),
            pltpu.VMEM((share, n_tok), bf16),
            pltpu.VMEM((share,), bf16),
            pltpu.VMEM((n_tok, share), bf16),
            pltpu.VMEM((n_tok, share), bf16),
            pltpu.VMEM((half - 1, split, voc_cols), bf16),
            pltpu.VMEM((half - 1, split, voc_cols), bf16),
            pltpu.VMEM((half - 1, n_tok - split, voc_cols), bf16),
            pltpu.VMEM((half - 1, n_tok - split, voc_cols), bf16),
            pltpu.VMEM((share, n_tok), bf16),
            pltpu.VMEM((groups - 1, share, n_tok), bf16),
            pltpu.VMEM((share, n_tok), f32),
            pltpu.VMEM((1, n_tok), f32),
            pltpu.VMEM((half - 1, 1, n_tok), f32),
            pltpu.VMEM((2, 2, n_tok), f32),
            pltpu.VMEM((nz - 1 + near, 2, n_tok), f32),
            pltpu.SemaphoreType.DMA((2,)),
            pltpu.SemaphoreType.DMA((n_copies,)),
            pltpu.SemaphoreType.DMA((n_copies,)),
        ],
        compiler_params=pltpu.CompilerParams(
            collective_id=0, has_side_effects=True, vmem_limit_bytes=60 * 1024 * 1024
        ),
    )(table, hidden.T, gain, ids)
    next_embed, logprobs, chosen = pl.pallas_call(
        finish,
        out_shape=(
            jax.ShapeDtypeStruct((share, n_tok), bf16),
            jax.ShapeDtypeStruct((n_tok, voc_cols), f32),
            jax.ShapeDtypeStruct((1, n_tok), f32),
        ),
        in_specs=[vmem] * 3,
        out_specs=(vmem,) * 3,
    )(embed, capped, stats)
    return (next_embed.T, logprobs, chosen[0])


def solution(mesh):
    placed = (P("vocab", "group"), P(None, "vocab"), P("vocab"), P())
    return jax.shard_map(
        body,
        mesh=mesh,
        in_specs=placed,
        out_specs=(P(None, "vocab"), P(None, ("group", "vocab")), P()),
        check_vma=False,
    )
```

```python
import functools
import math

import jax
import jax.numpy as jnp
from jax import lax
from jax.experimental import pallas as pl
from jax.experimental.pallas import tpu as pltpu
from jax.sharding import PartitionSpec as P

MESH = pl.DeviceIdType.MESH


def stage_bits(half, bits):
    dims = list(range(bits))
    if half == 0:
        dims[0], dims[1] = dims[1], dims[0]
    return [1 << d for d in dims]


def stage_of(half, mask, bits):
    for stage, bit in enumerate(stage_bits(half, bits)):
        if mask & bit:
            return stage
    return bits


def program_order(bits):
    if bits == 3:
        return [(1, 7), (0, 7), (0, 6), (1, 5), (0, 3), (0, 2), (0, 5), (1, 3), (1, 6), (0, 1), (1, 1),
                None, (1, 4), (0, 4), (1, 2)]
    every = [(half, mask) for mask in range((1 << bits) - 1, 0, -1) for half in (1, 0)]
    every.sort(key=lambda one: stage_of(one[0], one[1], bits))
    return every + [None]


def kernel(
    sizes, table, hidden, gain, ids, embed_out, capped_out, stats_out,
    tab_v, tpar, hown, hpar, gpar, own_n, par_n, send0, recv0, send1, recv1,
    xsend, xrecv, found, msend, mrecv, ssend, srecv, local_sem, send_sem, recv_sem,
):
    groups, share, width, n_tok, span, voc_cols, nz, bits, split = sizes
    f32, bf16 = jnp.float32, jnp.bfloat16
    g = lax.axis_index("group")
    v = lax.axis_index("vocab")
    c, y, z = v % 2, (v // 2) % 2, v // 4
    rows = ((0, split), (split, n_tok))
    sends, recvs = (send0, send1), (recv0, recv1)

    def flip(value, on):
        return 1 - value if on else value

    def place(mask, core):
        zz = 0
        for i in range(bits - 1):
            zz = zz + (1 << i) * flip((z // (1 << i)) % 2, (mask >> (i + 1)) & 1)
        return zz * 4 + flip(y, mask & 1) * 2 + core

    def z_peer(k):
        return (g, ((z + k) % nz) * 4 + y * 2 + c)

    def near_peer(d, m):
        gg = (g + d) % groups if d else g
        return (gg, z * 4 + flip(y, m & 1) * 2 + flip(c, m & 2))

    core_peer = near_peer(0, 2)
    z_peers = [z_peer(k) for k in range(1, nz)]
    near_all = [near_peer(0, m) for m in range(1, 4)] + [near_peer(d, m) for d in range(1, groups) for m in range(4)]

    def column(mask, core):
        return pl.ds(pl.multiple_of(place(mask, core) * voc_cols, 128), voc_cols)

    started = []

    def send(src, dst, peer):
        i = len(started)
        copy = pltpu.make_async_remote_copy(
            src_ref=src, dst_ref=dst, send_sem=send_sem.at[i], recv_sem=recv_sem.at[i],
            device_id=peer, device_id_type=MESH,
        )
        copy.start()
        started.append(copy)
        return copy

    h_load = pltpu.make_async_copy(hidden, hown, local_sem.at[0])
    h_load.start()
    load = pltpu.make_async_copy(table, tab_v, local_sem.at[1])
    load.start()

    barrier = pltpu.get_barrier_semaphore()
    chip_peers = [(g, place(m, c)) for m in range(1, 2 * nz)]
    everyone = chip_peers + [peer for m, peer in enumerate(near_all) if m != 0]
    for peer in everyone:
        pl.semaphore_signal(barrier, inc=1, device_id=peer, device_id_type=MESH)

    h_load.wait()
    states = hown[...].astype(f32)
    own_sq = jnp.sum(states * states, axis=0, keepdims=True)
    own_t = states.T * gain[...].astype(f32).reshape(1, share)
    pl.semaphore_wait(barrier, len(everyone))

    h_copy = send(hidden, hpar, core_peer)
    g_copy = send(gain, gpar, core_peer)
    order = program_order(bits)
    uses = []
    for one in order:
        if one and one[1] not in uses:
            uses.append(one[1])
    t_copies = {}
    for mask in uses + [0]:
        t_copies[mask] = send(table.at[:, column(mask, 1 - c)], tpar.at[mask], core_peer)

    h_copy.wait_recv()
    states = hpar[...].astype(f32)
    chip_sq = own_sq + jnp.sum(states * states, axis=0, keepdims=True)
    msend[...] = chip_sq
    sq_copies = [send(msend, mrecv.at[j], peer) for j, peer in enumerate(chip_peers)]

    def to_columns(row_list):
        full = jnp.concatenate(row_list + [row_list[0]] * (8 - len(row_list)), axis=0)
        full = full.T
        return [full[:, i:i + 1] for i in range(len(row_list))]

    chip_scale = to_columns([lax.rsqrt(chip_sq / width + 1e-06)])[0]
    own_n[...] = (own_t * chip_scale).astype(bf16)
    g_copy.wait_recv()
    par_t = states.T * gpar[...].astype(f32).reshape(1, share)
    par_n[...] = (par_t * chip_scale).astype(bf16)
    load.wait()

    ratios = []

    def ratio_columns():
        if not ratios:
            total = chip_sq
            for j, copy in enumerate(sq_copies):
                copy.wait_recv()
                total = total + mrecv[j]
            scale = lax.rsqrt(total / width + 1e-06)
            parts = [chip_sq, mrecv[0], mrecv[1]]
            ratios.extend(to_columns([
                jnp.where(scale == 0.0, 0.0, scale * jnp.sqrt(part / width + 1e-06))
                for part in parts]))
        return ratios

    landed = set()

    def partial(half, mask):
        if mask not in landed:
            t_copies[mask].wait_recv()
            landed.add(mask)
        low, high = rows[half]
        first = jnp.dot(own_n[low:high], tab_v[:, column(mask, c)], preferred_element_type=f32)
        return first + jnp.dot(par_n[low:high], tpar[mask], preferred_element_type=f32)

    arrivals = {}

    def reduced(half, mask):
        total = partial(half, mask)
        stage = stage_of(half, mask, bits)
        if stage == 0:
            return total
        low, high = rows[half]
        own, by_y, by_z = ratio_columns()
        total = total * own[low:high]
        for i, bit in enumerate(stage_bits(half, bits)[:stage]):
            arrivals[half, mask | bit].wait_recv()
            more = recvs[half][(mask | bit) - 1].astype(f32)
            if i == 0:
                more = more * (by_y if half else by_z)[low:high]
            total = total + more
        return total

    chunk = 2 * voc_cols
    local_ids = ids[...].reshape(1, n_tok) - g * span

    def gather(n, carry):
        start = n * chunk
        spots = lax.broadcasted_iota(jnp.int32, (chunk, n_tok), 0)
        hot = jnp.where(spots == local_ids - start, 1.0, 0.0).astype(bf16)
        found[...] += jnp.dot(tab_v[:, pl.ds(pl.multiple_of(start, 128), chunk)], hot,
                              preferred_element_type=f32)
        return carry

    x_copies = []
    for one in order:
        if one is None:
            found[...] = jnp.zeros_like(found)
            lax.fori_loop(0, span // chunk, gather, 0)
            xsend[...] = found[...].astype(bf16)
            x_copies = [send(xsend, xrecv.at[d - 1], near_peer(d, 0)) for d in range(1, groups)]
            continue
        half, mask = one
        sends[half][mask - 1] = reduced(half, mask).astype(bf16)
        bit = stage_bits(half, bits)[stage_of(half, mask, bits)]
        peer = (g, place(bit, c))
        arrivals[half, mask] = send(sends[half].at[mask - 1], recvs[half].at[mask - 1], peer)

    embed = found[...]
    for d, copy in enumerate(x_copies):
        copy.wait_recv()
        embed = embed + xrecv[d].astype(f32)
    embed_out[...] = (embed * math.sqrt(width)).astype(bf16)

    first_col = (g * 4 * nz + v) * voc_cols
    offsets = jnp.broadcast_to(ids[...].reshape(1, n_tok), (8, n_tok)).astype(f32).T[:, :1].astype(jnp.int32)
    sums, picks = [], []
    for half, (low, high) in enumerate(rows):
        capped = 30.0 * jnp.tanh(reduced(half, 0) / 30.0)
        capped_out[low:high] = capped
        spots = lax.broadcasted_iota(jnp.int32, capped.shape, 1)
        pick = jnp.where(spots == offsets[low:high] - first_col, capped, 0.0)
        sums.append(jnp.sum(jnp.exp(capped), axis=1, keepdims=True))
        picks.append(jnp.sum(pick, axis=1, keepdims=True))
    both = [jnp.broadcast_to(jnp.concatenate(one, axis=0), (n_tok, 8)).T[:1] for one in (sums, picks)]
    both = jnp.concatenate(both, axis=0)
    slot = 0
    for phase, peers in enumerate((z_peers, near_all)):
        ssend[phase] = both
        copies = []
        for peer in peers:
            copies.append((slot, send(ssend.at[phase], srecv.at[slot], peer)))
            slot += 1
        for at, copy in copies:
            copy.wait_recv()
            both = both + srecv[at]
    stats_out[...] = both
    for copy in started:
        copy.wait_send()


def finish(embed, capped, stats, embed_out, logprobs_out, chosen_out):
    log_total = jnp.log(stats[0:1])
    embed_out[...] = embed[...]
    logprobs_out[...] = capped[...] - jnp.broadcast_to(log_total, (8, log_total.shape[1])).T[:, :1]
    chosen_out[...] = stats[1:2] - log_total


def body(table, hidden, gain, ids):
    share, span = table.shape
    n_tok = hidden.shape[0]
    vocab_n = lax.axis_size("vocab")
    groups = lax.axis_size("group")
    voc_cols = span // vocab_n
    width = share * vocab_n
    nz = vocab_n // 4
    half = vocab_n // 2
    bits = half.bit_length() - 1
    split = n_tok // 64 * 16
    near = 3 + 4 * (groups - 1)
    n_copies = 2 + half + 3 * (half - 1) + (groups - 1) + (nz - 1) + near
    bf16, f32 = jnp.bfloat16, jnp.float32
    sizes = (groups, share, width, n_tok, span, voc_cols, nz, bits, split)
    vmem = pl.BlockSpec(memory_space=pltpu.VMEM)
    anywhere = pl.BlockSpec(memory_space=pltpu.HBM)
    embed, capped, stats = pl.pallas_call(
        functools.partial(kernel, sizes),
        out_shape=(
            jax.ShapeDtypeStruct((share, n_tok), bf16),
            jax.ShapeDtypeStruct((n_tok, voc_cols), f32),
            jax.ShapeDtypeStruct((2, n_tok), f32),
        ),
        in_specs=[anywhere, anywhere, vmem, vmem],
        out_specs=(vmem, vmem, vmem),
        scratch_shapes=[
            pltpu.VMEM((share, span), bf16),
            pltpu.VMEM((half, share, voc_cols), bf16),
            pltpu.VMEM((share, n_tok), bf16),
            pltpu.VMEM((share, n_tok), bf16),
            pltpu.VMEM((share,), bf16),
            pltpu.VMEM((n_tok, share), bf16),
            pltpu.VMEM((n_tok, share), bf16),
            pltpu.VMEM((half - 1, split, voc_cols), bf16),
            pltpu.VMEM((half - 1, split, voc_cols), bf16),
            pltpu.VMEM((half - 1, n_tok - split, voc_cols), bf16),
            pltpu.VMEM((half - 1, n_tok - split, voc_cols), bf16),
            pltpu.VMEM((share, n_tok), bf16),
            pltpu.VMEM((groups - 1, share, n_tok), bf16),
            pltpu.VMEM((share, n_tok), f32),
            pltpu.VMEM((1, n_tok), f32),
            pltpu.VMEM((half - 1, 1, n_tok), f32),
            pltpu.VMEM((2, 2, n_tok), f32),
            pltpu.VMEM((nz - 1 + near, 2, n_tok), f32),
            pltpu.SemaphoreType.DMA((2,)),
            pltpu.SemaphoreType.DMA((n_copies,)),
            pltpu.SemaphoreType.DMA((n_copies,)),
        ],
        compiler_params=pltpu.CompilerParams(
            collective_id=0, has_side_effects=True, vmem_limit_bytes=52 * 1024 * 1024
        ),
    )(table, hidden.T, gain, ids)
    next_embed, logprobs, chosen = pl.pallas_call(
        finish,
        out_shape=(
            jax.ShapeDtypeStruct((share, n_tok), bf16),
            jax.ShapeDtypeStruct((n_tok, voc_cols), f32),
            jax.ShapeDtypeStruct((1, n_tok), f32),
        ),
        in_specs=[vmem] * 3,
        out_specs=(vmem,) * 3,
        compiler_params=pltpu.CompilerParams(vmem_limit_bytes=8 * 1024 * 1024),
    )(embed, capped, stats)
    return (next_embed.T, logprobs, chosen[0])


def solution(mesh):
    placed = (P("vocab", "group"), P(None, "vocab"), P("vocab"), P())
    return jax.shard_map(
        body,
        mesh=mesh,
        in_specs=placed,
        out_specs=(P(None, "vocab"), P(None, ("group", "vocab")), P()),
        check_vma=False,
    )
```

```python
import functools
import math

import jax
import jax.numpy as jnp
from jax import lax
from jax.experimental import pallas as pl
from jax.experimental.pallas import tpu as pltpu
from jax.sharding import PartitionSpec as P

MESH = pl.DeviceIdType.MESH


def stage_bits(half, bits):
    dims = list(range(bits))
    if half == 0:
        dims[0], dims[1] = dims[1], dims[0]
    return [1 << d for d in dims]


def stage_of(half, mask, bits):
    for stage, bit in enumerate(stage_bits(half, bits)):
        if mask & bit:
            return stage
    return bits


def program_order(bits):
    if bits == 3:
        return [(0, 7), (1, 7), (0, 6), (1, 5), (0, 3), (0, 2), (0, 5), (1, 3), (1, 6), (0, 1), (1, 1),
                None, (0, 4), (1, 4), (1, 2)]
    every = [(half, mask) for mask in range((1 << bits) - 1, 0, -1) for half in (1, 0)]
    every.sort(key=lambda one: stage_of(one[0], one[1], bits))
    return every + [None]


def kernel(
    sizes, table, hidden, gain, ids, embed_out, capped_out, stats_out,
    tab_v, tpar, hown, hpar, gpar, own_n, par_n, send0, recv0, send1, recv1,
    xsend, xrecv, found, msend, mrecv, ssend, srecv, local_sem, send_sem, recv_sem,
):
    groups, share, width, n_tok, span, voc_cols, nz, bits, split = sizes
    f32, bf16 = jnp.float32, jnp.bfloat16
    g = lax.axis_index("group")
    v = lax.axis_index("vocab")
    c, y, z = v % 2, (v // 2) % 2, v // 4
    rows = ((0, split), (split, n_tok))
    sends, recvs = (send0, send1), (recv0, recv1)

    def flip(value, on):
        return 1 - value if on else value

    def place(mask, core):
        zz = 0
        for i in range(bits - 1):
            zz = zz + (1 << i) * flip((z // (1 << i)) % 2, (mask >> (i + 1)) & 1)
        return zz * 4 + flip(y, mask & 1) * 2 + core

    def z_peer(k):
        return (g, ((z + k) % nz) * 4 + y * 2 + c)

    def near_peer(d, m):
        gg = (g + d) % groups if d else g
        return (gg, z * 4 + flip(y, m & 1) * 2 + flip(c, m & 2))

    core_peer = near_peer(0, 2)
    z_peers = [z_peer(k) for k in range(1, nz)]
    near_all = [near_peer(0, m) for m in range(1, 4)] + [near_peer(d, m) for d in range(1, groups) for m in range(4)]

    def column(mask, core):
        return pl.ds(pl.multiple_of(place(mask, core) * voc_cols, 128), voc_cols)

    started = []

    def send(src, dst, peer):
        i = len(started)
        copy = pltpu.make_async_remote_copy(
            src_ref=src, dst_ref=dst, send_sem=send_sem.at[i], recv_sem=recv_sem.at[i],
            device_id=peer, device_id_type=MESH,
        )
        copy.start()
        started.append(copy)
        return copy

    h_load = pltpu.make_async_copy(hidden, hown, local_sem.at[0])
    h_load.start()
    load = pltpu.make_async_copy(table, tab_v, local_sem.at[1])
    load.start()

    barrier = pltpu.get_barrier_semaphore()
    chip_peers = [(g, place(m, c)) for m in range(1, 2 * nz)]
    everyone = chip_peers + [peer for m, peer in enumerate(near_all) if m != 0]
    for peer in everyone:
        pl.semaphore_signal(barrier, inc=1, device_id=peer, device_id_type=MESH)

    h_load.wait()
    states = hown[...].astype(f32)
    own_sq = jnp.sum(states * states, axis=0, keepdims=True)
    own_t = states.T * gain[...].astype(f32).reshape(1, share)
    pl.semaphore_wait(barrier, len(everyone))

    h_copy = send(hidden, hpar, core_peer)
    g_copy = send(gain, gpar, core_peer)
    order = program_order(bits)
    uses = []
    for one in order:
        if one and one[1] not in uses:
            uses.append(one[1])
    t_copies = {}
    for mask in uses + [0]:
        t_copies[mask] = send(table.at[:, column(mask, 1 - c)], tpar.at[mask], core_peer)

    h_copy.wait_recv()
    states = hpar[...].astype(f32)
    chip_sq = own_sq + jnp.sum(states * states, axis=0, keepdims=True)
    msend[...] = chip_sq
    sq_copies = [send(msend, mrecv.at[j], peer) for j, peer in enumerate(chip_peers)]

    def to_columns(row_list):
        full = jnp.concatenate(row_list + [row_list[0]] * (8 - len(row_list)), axis=0)
        full = full.T
        return [full[:, i:i + 1] for i in range(len(row_list))]

    chip_scale = to_columns([lax.rsqrt(chip_sq / width + 1e-06)])[0]
    own_n[...] = (own_t * chip_scale).astype(bf16)
    g_copy.wait_recv()
    par_t = states.T * gpar[...].astype(f32).reshape(1, share)
    par_n[...] = (par_t * chip_scale).astype(bf16)
    load.wait()

    ratios = []

    def ratio_columns():
        if not ratios:
            total = chip_sq
            for j, copy in enumerate(sq_copies):
                copy.wait_recv()
                total = total + mrecv[j]
            scale = lax.rsqrt(total / width + 1e-06)
            parts = [chip_sq, mrecv[0], mrecv[1]]
            ratios.extend(to_columns([
                jnp.where(scale == 0.0, 0.0, scale * jnp.sqrt(part / width + 1e-06))
                for part in parts]))
        return ratios

    landed = set()

    def partial(half, mask):
        if mask not in landed:
            t_copies[mask].wait_recv()
            landed.add(mask)
        low, high = rows[half]
        first = jnp.dot(own_n[low:high], tab_v[:, column(mask, c)], preferred_element_type=f32)
        return first + jnp.dot(par_n[low:high], tpar[mask], preferred_element_type=f32)

    arrivals = {}

    def reduced(half, mask):
        total = partial(half, mask)
        stage = stage_of(half, mask, bits)
        if stage == 0:
            return total
        low, high = rows[half]
        own, by_y, by_z = ratio_columns()
        total = total * own[low:high]
        for i, bit in enumerate(stage_bits(half, bits)[:stage]):
            arrivals[half, mask | bit].wait_recv()
            more = recvs[half][(mask | bit) - 1].astype(f32)
            if i == 0:
                more = more * (by_y if half else by_z)[low:high]
            total = total + more
        return total

    chunk = 2 * voc_cols
    local_ids = ids[...].reshape(1, n_tok) - g * span

    def gather(n, carry):
        start = n * chunk
        spots = lax.broadcasted_iota(jnp.int32, (chunk, n_tok), 0)
        hot = jnp.where(spots == local_ids - start, 1.0, 0.0).astype(bf16)
        found[...] += jnp.dot(tab_v[:, pl.ds(pl.multiple_of(start, 128), chunk)], hot,
                              preferred_element_type=f32)
        return carry

    x_copies = []
    for one in order:
        if one is None:
            found[...] = jnp.zeros_like(found)
            lax.fori_loop(0, span // chunk, gather, 0)
            xsend[...] = found[...].astype(bf16)
            x_copies = [send(xsend, xrecv.at[d - 1], near_peer(d, 0)) for d in range(1, groups)]
            continue
        half, mask = one
        sends[half][mask - 1] = reduced(half, mask).astype(bf16)
        bit = stage_bits(half, bits)[stage_of(half, mask, bits)]
        peer = (g, place(bit, c))
        arrivals[half, mask] = send(sends[half].at[mask - 1], recvs[half].at[mask - 1], peer)

    embed = found[...]
    for d, copy in enumerate(x_copies):
        copy.wait_recv()
        embed = embed + xrecv[d].astype(f32)
    embed_out[...] = (embed * math.sqrt(width)).astype(bf16)

    first_col = (g * 4 * nz + v) * voc_cols
    offsets = jnp.broadcast_to(ids[...].reshape(1, n_tok), (8, n_tok)).astype(f32).T[:, :1].astype(jnp.int32)
    sums, picks = [], []
    for half, (low, high) in enumerate(rows):
        capped = 30.0 * jnp.tanh(reduced(half, 0) / 30.0)
        capped_out[low:high] = capped
        spots = lax.broadcasted_iota(jnp.int32, capped.shape, 1)
        pick = jnp.where(spots == offsets[low:high] - first_col, capped, 0.0)
        sums.append(jnp.sum(jnp.exp(capped), axis=1, keepdims=True))
        picks.append(jnp.sum(pick, axis=1, keepdims=True))
    both = [jnp.broadcast_to(jnp.concatenate(one, axis=0), (n_tok, 8)).T[:1] for one in (sums, picks)]
    both = jnp.concatenate(both, axis=0)
    slot = 0
    for phase, peers in enumerate((z_peers, near_all)):
        ssend[phase] = both
        copies = []
        for peer in peers:
            copies.append((slot, send(ssend.at[phase], srecv.at[slot], peer)))
            slot += 1
        for at, copy in copies:
            copy.wait_recv()
            both = both + srecv[at]
    stats_out[...] = both
    for copy in started:
        copy.wait_send()


def finish(embed, capped, stats, embed_out, logprobs_out, chosen_out):
    log_total = jnp.log(stats[0:1])
    embed_out[...] = embed[...]
    logprobs_out[...] = capped[...] - jnp.broadcast_to(log_total, (8, log_total.shape[1])).T[:, :1]
    chosen_out[...] = stats[1:2] - log_total


def body(table, hidden, gain, ids):
    share, span = table.shape
    n_tok = hidden.shape[0]
    vocab_n = lax.axis_size("vocab")
    groups = lax.axis_size("group")
    voc_cols = span // vocab_n
    width = share * vocab_n
    nz = vocab_n // 4
    half = vocab_n // 2
    bits = half.bit_length() - 1
    split = n_tok // 112 * 32
    near = 3 + 4 * (groups - 1)
    n_copies = 2 + half + 3 * (half - 1) + (groups - 1) + (nz - 1) + near
    bf16, f32 = jnp.bfloat16, jnp.float32
    sizes = (groups, share, width, n_tok, span, voc_cols, nz, bits, split)
    vmem = pl.BlockSpec(memory_space=pltpu.VMEM)
    anywhere = pl.BlockSpec(memory_space=pltpu.HBM)
    embed, capped, stats = pl.pallas_call(
        functools.partial(kernel, sizes),
        out_shape=(
            jax.ShapeDtypeStruct((share, n_tok), bf16),
            jax.ShapeDtypeStruct((n_tok, voc_cols), f32),
            jax.ShapeDtypeStruct((2, n_tok), f32),
        ),
        in_specs=[anywhere, anywhere, vmem, vmem],
        out_specs=(vmem, vmem, vmem),
        scratch_shapes=[
            pltpu.VMEM((share, span), bf16),
            pltpu.VMEM((half, share, voc_cols), bf16),
            pltpu.VMEM((share, n_tok), bf16),
            pltpu.VMEM((share, n_tok), bf16),
            pltpu.VMEM((share,), bf16),
            pltpu.VMEM((n_tok, share), bf16),
            pltpu.VMEM((n_tok, share), bf16),
            pltpu.VMEM((half - 1, split, voc_cols), bf16),
            pltpu.VMEM((half - 1, split, voc_cols), bf16),
            pltpu.VMEM((half - 1, n_tok - split, voc_cols), bf16),
            pltpu.VMEM((half - 1, n_tok - split, voc_cols), bf16),
            pltpu.VMEM((share, n_tok), bf16),
            pltpu.VMEM((groups - 1, share, n_tok), bf16),
            pltpu.VMEM((share, n_tok), f32),
            pltpu.VMEM((1, n_tok), f32),
            pltpu.VMEM((half - 1, 1, n_tok), f32),
            pltpu.VMEM((2, 2, n_tok), f32),
            pltpu.VMEM((nz - 1 + near, 2, n_tok), f32),
            pltpu.SemaphoreType.DMA((2,)),
            pltpu.SemaphoreType.DMA((n_copies,)),
            pltpu.SemaphoreType.DMA((n_copies,)),
        ],
        compiler_params=pltpu.CompilerParams(
            collective_id=0, has_side_effects=True, vmem_limit_bytes=52 * 1024 * 1024
        ),
    )(table, hidden.T, gain, ids)
    next_embed, logprobs, chosen = pl.pallas_call(
        finish,
        out_shape=(
            jax.ShapeDtypeStruct((share, n_tok), bf16),
            jax.ShapeDtypeStruct((n_tok, voc_cols), f32),
            jax.ShapeDtypeStruct((1, n_tok), f32),
        ),
        in_specs=[vmem] * 3,
        out_specs=(vmem,) * 3,
        compiler_params=pltpu.CompilerParams(vmem_limit_bytes=8 * 1024 * 1024),
    )(embed, capped, stats)
    return (next_embed.T, logprobs, chosen[0])


def solution(mesh):
    placed = (P("vocab", "group"), P(None, "vocab"), P("vocab"), P())
    return jax.shard_map(
        body,
        mesh=mesh,
        in_specs=placed,
        out_specs=(P(None, "vocab"), P(None, ("group", "vocab")), P()),
        check_vma=False,
    )
```
